32 devices in a mesh: occ: 8 (over z, x), virt: 4 (over y, core).
Axes of the slice: x: 2, y: 2, z: 4, core: 2. Of those that a mesh axis runs over, the one named last changes fastest.
Arguments:
- factors: float32 [64, 512, 512], P('occ'), may hold values from -0.9 to 0.9
- occ_energy: float32 [64], replicated, may hold values from -3 to -0.5
- virt_energy: float32 [512], replicated, may hold values from 0.5 to 9.5
- pairing: int32 [2, 8], replicated, may hold values from 0 to 7, as said below
Outputs:
- pair_energy: float32 [2, 64], P(None, 'occ')
- gradient: float32 [64, 512, 512], P('occ', 'virt')
The draws below stay inside these ranges and needn't reach their ends.
Inputs may be any that keep to these rules, and one draw needn't show every extreme that they name: `pairing`: in every round each group's partner is another group whose partner is that group.
All inputs are finite; a program needn't handle non-finite values.
Results may differ from the reference program's by a relative error of at most 0.0001.
Values sent between devices are 32-bit elements; how exact they have to be, the bound alone decides.
A program may use at most 192 MiB of HBM per device.

```python
import jax
import jax.numpy as jnp
from jax import lax

OG = 8
V = 512
NAUX = 512
ROUNDS = 2
GROUPS = 8
NOCC = 64


def draw_virt_energy(key, part):
    increments = jax.random.uniform(jax.random.fold_in(key, 7), (V,), jnp.float32, 0.5, 1.5) * (6.0 / V)
    return (0.5 + jnp.cumsum(increments)).astype(jnp.float32)


def draw_pairing(key, part):
    plan = []
    for round_index in range(ROUNDS):
        shuffled = jax.random.permutation(jax.random.fold_in(key, 11 + round_index), GROUPS).astype(jnp.int32)
        positions = jnp.arange(GROUPS, dtype=jnp.int32) ^ 1
        mates = shuffled[positions]
        partner_row = jnp.zeros((GROUPS,), jnp.int32).at[shuffled].set(mates)
        plan.append(partner_row)
    return jnp.stack(plan).astype(jnp.int32)


def block_scale(key, dims, split, low, largest):
    loudness, own = 1.0, jax.random.fold_in(key, 6)
    for dim, blocks in split:
        steps = jnp.exp(jax.random.uniform(jax.random.fold_in(own, dim), (blocks,), jnp.float32, low / len(split), largest / len(split)))
        loudness = loudness * jnp.repeat(steps, dims[dim] // blocks).reshape([-1 if axis == dim else 1 for axis in range(len(dims))])
    return loudness


def centred(own_key, dims, spread, most, cuts=(), held_as=jnp.bfloat16):
    result = jax.random.normal(own_key, dims, jnp.float32) * spread
    if len(cuts) > 0:
        result = block_scale(own_key, dims, cuts, -0.22, 0.18) * result
    return jnp.clip(result, min=-most, max=most).astype(held_as)


def setup_inputs(seed: int = 0) -> dict:
    streams_of = jax.random.split(jax.random.key(seed), 5)
    factors = centred(streams_of[0], (NOCC, V, NAUX), 0.15, 0.9, ((0, 8),), jnp.float32)
    occ_energy = jnp.clip(jax.random.uniform(streams_of[1], (NOCC,), jnp.float32, -3.0, -0.5), -3.0, -0.5)
    virt_energy = draw_virt_energy(jax.random.fold_in(streams_of[4], 71), 0)
    pairing = draw_pairing(jax.random.fold_in(streams_of[4], 71), 0)
    return dict(factors=factors, occ_energy=occ_energy, virt_energy=virt_energy, pairing=pairing)


def pair_block(own_part, mate_part, own_energy, mate_energy, virt_energy):
    highest = lax.Precision.HIGHEST
    coulomb = jnp.einsum('iap,jbp->iajb', own_part, mate_part, precision=highest)
    swapped = jnp.einsum('ibp,jap->iajb', own_part, mate_part, precision=highest)
    denominator = (virt_energy[None, :, None, None] + virt_energy[None, None, None, :]
                   - own_energy[:, None, None, None] - mate_energy[None, None, :, None])
    amplitude = -(2.0 * coulomb - swapped) / denominator
    energy = jnp.sum(amplitude * coulomb, axis=(1, 2, 3)) / (V * OG * V)
    grad_part = jnp.einsum('iajb,jbp->iap', amplitude, mate_part, precision=highest)
    return energy, grad_part


def reference(factors, occ_energy, virt_energy, pairing):
    grouped = factors.reshape(GROUPS, OG, V, NAUX)
    grouped_energy = occ_energy.reshape(GROUPS, OG)
    total_grad = jnp.zeros((GROUPS, OG, V, NAUX), jnp.float32)
    energy_rows = []
    for round_index in range(ROUNDS):
        def one_group(group_index):
            mate_index = pairing[round_index, group_index]
            return pair_block(grouped[group_index], grouped[mate_index],
                              grouped_energy[group_index], grouped_energy[mate_index], virt_energy)
        energy_now, grad_now = lax.map(one_group, jnp.arange(GROUPS, dtype=jnp.int32))
        total_grad = total_grad + grad_now
        energy_rows.append(energy_now.reshape(NOCC))
    return jnp.stack(energy_rows), total_grad.reshape(NOCC, V, NAUX)
```

```python
import functools

import jax
import jax.numpy as jnp
from jax import lax
from jax.experimental import pallas as pl
from jax.experimental.pallas import tpu as pltpu
from jax.sharding import PartitionSpec as P

OG = 8
V = 512
ROUNDS = 2


def block_amplitude(
    own_rows, mate_rows, own_piece, fragment, own_energy, mate_energy, energy_left, energy_right
):
    highest = lax.Precision.HIGHEST
    groups_rows, slab_width, naux_width = own_rows.shape
    frag_width = fragment.shape[1]
    contract = (((1,), (1,)), ((), ()))
    coulomb = lax.dot_general(
        own_rows.reshape(groups_rows * slab_width, naux_width),
        fragment.reshape(groups_rows * frag_width, naux_width),
        contract,
        precision=highest,
        preferred_element_type=jnp.float32,
    )
    coulomb = coulomb.reshape(groups_rows, slab_width, groups_rows, frag_width)
    swapped = lax.dot_general(
        own_piece.reshape(groups_rows * frag_width, naux_width),
        mate_rows.reshape(groups_rows * slab_width, naux_width),
        contract,
        precision=highest,
        preferred_element_type=jnp.float32,
    )
    swapped = swapped.reshape(groups_rows, frag_width, groups_rows, slab_width).transpose(
        0, 3, 2, 1
    )
    denominator = (
        energy_left[None, :, None, None]
        + energy_right[None, None, None, :]
        - own_energy[:, None, None, None]
        - mate_energy[None, None, :, None]
    )
    amplitude = -(2.0 * coulomb - swapped) / denominator
    return (amplitude, coulomb)


def block_terms(
    own_rows, mate_rows, own_piece, fragment, own_energy, mate_energy, energy_left, energy_right
):
    highest = lax.Precision.HIGHEST
    groups_rows, slab_width, naux_width = own_rows.shape
    frag_width = fragment.shape[1]
    amplitude, coulomb = block_amplitude(
        own_rows, mate_rows, own_piece, fragment, own_energy, mate_energy, energy_left, energy_right
    )
    energy = jnp.sum(amplitude * coulomb, axis=(1, 2, 3))
    grad_part = jnp.dot(
        amplitude.reshape(groups_rows * slab_width, groups_rows * frag_width),
        fragment.reshape(groups_rows * frag_width, naux_width),
        precision=highest,
        preferred_element_type=jnp.float32,
    )
    return (energy, grad_part)


def route_slab(own_rows, partner_row, group_count):
    groups_rows, slab_width, naux_width = own_rows.shape
    split_rows = own_rows.reshape(group_count, groups_rows * slab_width // group_count, naux_width)
    mixed = lax.all_to_all(split_rows, "occ", split_axis=0, concat_axis=0, tiled=True)
    ordered = jnp.take(mixed, partner_row, axis=0)
    arrived = lax.all_to_all(ordered, "occ", split_axis=0, concat_axis=0, tiled=True)
    return arrived.reshape(groups_rows, slab_width, naux_width)


def per_device_slabs(factors, occ_energy, virt_energy, pairing):
    group_index = lax.axis_index("occ")
    column_index = lax.axis_index("virt")
    group_count = lax.axis_size("occ")
    virt_count = lax.axis_size("virt")
    groups_rows, virt_width, naux_width = factors.shape
    slab_width = virt_width // virt_count
    own_rows = lax.dynamic_slice_in_dim(factors, column_index * slab_width, slab_width, 1)
    own_energy = lax.dynamic_slice_in_dim(occ_energy, group_index * groups_rows, groups_rows, 0)
    energy_left = lax.dynamic_slice_in_dim(virt_energy, column_index * slab_width, slab_width, 0)
    total_grad = jnp.zeros((groups_rows * slab_width, naux_width), jnp.float32)
    energy_rows = []
    for round_index in range(ROUNDS):
        partner_row = pairing[round_index]
        mate_index = partner_row[group_index]
        mate_energy = lax.dynamic_slice_in_dim(occ_energy, mate_index * groups_rows, groups_rows, 0)
        partner_row, mate_energy = (partner_row, mate_energy)
        mate_rows = route_slab(own_rows, partner_row, group_count)

        def fold_step(carry, fragment, offset, mate_rows=mate_rows, mate_energy=mate_energy):
            own_piece, energy_right = (factors, virt_energy)
            energy, grad_part = block_terms(
                own_rows,
                mate_rows,
                own_piece,
                fragment,
                own_energy,
                mate_energy,
                energy_left,
                energy_right,
            )
            return (carry[0] + grad_part, energy)

        total_grad, energy_now = fold_step(
            (total_grad, jnp.zeros((groups_rows,), jnp.float32)),
            lax.all_gather(mate_rows, "virt", axis=1, tiled=True),
            jnp.int32(0),
        )
        energy_rows.append(energy_now)
    stacked = jnp.stack(energy_rows)
    stacked = stacked / (V * OG * V)
    pair_energy = lax.psum(stacked, "virt")
    return (pair_energy, total_grad.reshape(groups_rows, slab_width, naux_width))


CHUNKS = 4


def split_hi_lo(values):
    high = values.astype(jnp.bfloat16)
    low = (values - high.astype(jnp.float32)).astype(jnp.bfloat16)
    return high, low


def pair_kernel(
    mate_count,
    pairing_ref,
    occ_ref,
    own_ref,
    mates_ref,
    left_ref,
    right_ref,
    grad_ref,
    energy_ref,
    own_wide,
    mate_wide,
    mate_tall,
    amp_wide,
    total,
):
    row, step = pl.program_id(0), pl.program_id(1)
    steps = pl.num_programs(1)
    virt_width, naux_width = total.shape
    depth = naux_width

    @pl.when(row == 0)
    def _():
        high, low = split_hi_lo(mates_ref[0, 0])
        mate_wide[step, :, :depth] = high
        mate_wide[step, :, depth : 2 * depth] = high
        mate_wide[step, :, 2 * depth :] = low
        mate_tall[step, :virt_width] = high
        mate_tall[step, virt_width : 2 * virt_width] = high
        mate_tall[step, 2 * virt_width :] = low

    @pl.when(step == 0)
    def _():
        high, low = split_hi_lo(own_ref[0])
        own_wide[:, :depth] = high
        own_wide[:, depth : 2 * depth] = low
        own_wide[:, 2 * depth :] = high

    coulomb = lax.dot_general(
        own_wide[...],
        mate_wide[step],
        (((1,), (1,)), ((), ())),
        preferred_element_type=jnp.float32,
    )
    round_index, mate = step // mate_count, step % mate_count
    own_energy = occ_ref[0, row]
    mate_energy = occ_ref[1 + round_index, mate]
    denominator = left_ref[...] + right_ref[...] - own_energy - mate_energy
    amplitude = (coulomb.T - 2.0 * coulomb) / denominator
    energy_ref[0, 0] = (amplitude * coulomb).reshape(virt_width // 8, 8, virt_width).sum(0)
    high, low = split_hi_lo(amplitude)
    amp_wide[:, :virt_width] = high
    amp_wide[:, virt_width : 2 * virt_width] = low
    amp_wide[:, 2 * virt_width :] = high
    part = jnp.dot(amp_wide[...], mate_tall[step], preferred_element_type=jnp.float32)

    @pl.when(step == 0)
    def _():
        total[...] = part

    @pl.when(step > 0)
    def _():
        total[...] += part

    @pl.when(step == steps - 1)
    def _():
        grad_ref[0] = total[...]


def pair_rows(own, first, rows, mates, partners, energies, virt_energy):
    _, virt_width, naux_width = own.shape
    mate_count = mates.shape[1]
    rounds = partners.shape[0]
    steps = rounds * mate_count

    def mate_map(row, step, partners_ref, energies_ref):
        now = jnp.where(row == 0, step, steps - 1)
        return partners_ref[now // mate_count], now % mate_count, 0, 0

    flops = 2 * 2 * 3 * rows * steps * virt_width * virt_width * naux_width
    return pl.pallas_call(
        functools.partial(pair_kernel, mate_count),
        grid_spec=pltpu.PrefetchScalarGridSpec(
            num_scalar_prefetch=2,
            grid=(rows, steps),
            in_specs=[
                pl.BlockSpec((1, virt_width, naux_width), lambda i, s, p, e: (first + i, 0, 0)),
                pl.BlockSpec((1, 1, virt_width, naux_width), mate_map),
                pl.BlockSpec((virt_width, 1), lambda i, s, p, e: (0, 0)),
                pl.BlockSpec((1, virt_width), lambda i, s, p, e: (0, 0)),
            ],
            out_specs=[
                pl.BlockSpec((1, virt_width, naux_width), lambda i, s, p, e: (i, 0, 0)),
                pl.BlockSpec((1, 1, 8, virt_width), lambda i, s, p, e: (i, s, 0, 0)),
            ],
            scratch_shapes=[
                pltpu.VMEM((virt_width, 3 * naux_width), jnp.bfloat16),
                pltpu.VMEM((steps, virt_width, 3 * naux_width), jnp.bfloat16),
                pltpu.VMEM((steps, 3 * virt_width, naux_width), jnp.bfloat16),
                pltpu.VMEM((virt_width, 3 * virt_width), jnp.bfloat16),
                pltpu.VMEM((virt_width, naux_width), jnp.float32),
            ],
        ),
        out_shape=[
            jax.ShapeDtypeStruct((rows, virt_width, naux_width), jnp.float32),
            jax.ShapeDtypeStruct((rows, steps, 8, virt_width), jnp.float32),
        ],
        cost_estimate=pl.CostEstimate(flops=flops, bytes_accessed=2**24, transcendentals=0),
        name="pair_rows",
    )(partners, energies, own, mates, virt_energy[:, None], virt_energy[None, :])


def spread_mates(share):
    return lax.all_gather(share, "occ", axis=0, tiled=False)


def per_device(factors, occ_energy, virt_energy, pairing):
    group_index = lax.axis_index("occ")
    column_index = lax.axis_index("virt")
    virt_count = lax.axis_size("virt")
    groups_rows, virt_width, naux_width = factors.shape
    if groups_rows % virt_count or groups_rows % CHUNKS:
        return per_device_slabs(factors, occ_energy, virt_energy, pairing)
    mate_count = groups_rows // virt_count
    rounds = pairing.shape[0]
    share = lax.dynamic_slice_in_dim(factors, column_index * mate_count, mate_count, 0)
    mates = spread_mates(share)
    partners = pairing[:, group_index]
    grouped = occ_energy.reshape(-1, groups_rows)
    own_energy = grouped[group_index]
    mate_energy = lax.dynamic_slice_in_dim(
        grouped[partners], column_index * mate_count, mate_count, 1
    )
    rows = groups_rows // CHUNKS
    width = max(rows, mate_count)
    mate_energy = jnp.pad(mate_energy, ((0, 0), (0, width - mate_count)))
    energy_parts, grads = [], []
    for chunk in range(CHUNKS):
        picked = slice(chunk * rows, (chunk + 1) * rows)
        energies = jnp.pad(own_energy[None, picked], ((0, 0), (0, width - rows)))
        energies = jnp.concatenate([energies, mate_energy])
        grad, energy = pair_rows(factors, chunk * rows, rows, mates, partners, energies, virt_energy)
        grads.append(lax.psum_scatter(grad, "virt", scatter_dimension=1, tiled=True))
        energy = energy.reshape(rows, rounds, -1).sum(2).T
        energy_parts.append(energy)
    stacked = jnp.concatenate(energy_parts, axis=1) / (virt_width * groups_rows * virt_width)
    return lax.psum(stacked, "virt"), jnp.concatenate(grads, axis=0)


def solution(mesh):
    placed = (P("occ", None, None), P(), P(), P())
    return jax.shard_map(
        per_device,
        mesh=mesh,
        in_specs=placed,
        out_specs=(P(None, "occ"), P("occ", "virt", None)),
        check_vma=False,
    )
```

```python
import functools

import jax
import jax.numpy as jnp
from jax import lax
from jax.experimental import pallas as pl
from jax.experimental.pallas import tpu as pltpu
from jax.sharding import PartitionSpec as P

OG = 8
V = 512
ROUNDS = 2


def block_amplitude(
    own_rows, mate_rows, own_piece, fragment, own_energy, mate_energy, energy_left, energy_right
):
    highest = lax.Precision.HIGHEST
    groups_rows, slab_width, naux_width = own_rows.shape
    frag_width = fragment.shape[1]
    contract = (((1,), (1,)), ((), ()))
    coulomb = lax.dot_general(
        own_rows.reshape(groups_rows * slab_width, naux_width),
        fragment.reshape(groups_rows * frag_width, naux_width),
        contract,
        precision=highest,
        preferred_element_type=jnp.float32,
    )
    coulomb = coulomb.reshape(groups_rows, slab_width, groups_rows, frag_width)
    swapped = lax.dot_general(
        own_piece.reshape(groups_rows * frag_width, naux_width),
        mate_rows.reshape(groups_rows * slab_width, naux_width),
        contract,
        precision=highest,
        preferred_element_type=jnp.float32,
    )
    swapped = swapped.reshape(groups_rows, frag_width, groups_rows, slab_width).transpose(
        0, 3, 2, 1
    )
    denominator = (
        energy_left[None, :, None, None]
        + energy_right[None, None, None, :]
        - own_energy[:, None, None, None]
        - mate_energy[None, None, :, None]
    )
    amplitude = -(2.0 * coulomb - swapped) / denominator
    return (amplitude, coulomb)


def block_terms(
    own_rows, mate_rows, own_piece, fragment, own_energy, mate_energy, energy_left, energy_right
):
    highest = lax.Precision.HIGHEST
    groups_rows, slab_width, naux_width = own_rows.shape
    frag_width = fragment.shape[1]
    amplitude, coulomb = block_amplitude(
        own_rows, mate_rows, own_piece, fragment, own_energy, mate_energy, energy_left, energy_right
    )
    energy = jnp.sum(amplitude * coulomb, axis=(1, 2, 3))
    grad_part = jnp.dot(
        amplitude.reshape(groups_rows * slab_width, groups_rows * frag_width),
        fragment.reshape(groups_rows * frag_width, naux_width),
        precision=highest,
        preferred_element_type=jnp.float32,
    )
    return (energy, grad_part)


def route_slab(own_rows, partner_row, group_count):
    groups_rows, slab_width, naux_width = own_rows.shape
    split_rows = own_rows.reshape(group_count, groups_rows * slab_width // group_count, naux_width)
    mixed = lax.all_to_all(split_rows, "occ", split_axis=0, concat_axis=0, tiled=True)
    ordered = jnp.take(mixed, partner_row, axis=0)
    arrived = lax.all_to_all(ordered, "occ", split_axis=0, concat_axis=0, tiled=True)
    return arrived.reshape(groups_rows, slab_width, naux_width)


def per_device_slabs(factors, occ_energy, virt_energy, pairing):
    group_index = lax.axis_index("occ")
    column_index = lax.axis_index("virt")
    group_count = lax.axis_size("occ")
    virt_count = lax.axis_size("virt")
    groups_rows, virt_width, naux_width = factors.shape
    slab_width = virt_width // virt_count
    own_rows = lax.dynamic_slice_in_dim(factors, column_index * slab_width, slab_width, 1)
    own_energy = lax.dynamic_slice_in_dim(occ_energy, group_index * groups_rows, groups_rows, 0)
    energy_left = lax.dynamic_slice_in_dim(virt_energy, column_index * slab_width, slab_width, 0)
    total_grad = jnp.zeros((groups_rows * slab_width, naux_width), jnp.float32)
    energy_rows = []
    for round_index in range(ROUNDS):
        partner_row = pairing[round_index]
        mate_index = partner_row[group_index]
        mate_energy = lax.dynamic_slice_in_dim(occ_energy, mate_index * groups_rows, groups_rows, 0)
        partner_row, mate_energy = (partner_row, mate_energy)
        mate_rows = route_slab(own_rows, partner_row, group_count)

        def fold_step(carry, fragment, offset, mate_rows=mate_rows, mate_energy=mate_energy):
            own_piece, energy_right = (factors, virt_energy)
            energy, grad_part = block_terms(
                own_rows,
                mate_rows,
                own_piece,
                fragment,
                own_energy,
                mate_energy,
                energy_left,
                energy_right,
            )
            return (carry[0] + grad_part, energy)

        total_grad, energy_now = fold_step(
            (total_grad, jnp.zeros((groups_rows,), jnp.float32)),
            lax.all_gather(mate_rows, "virt", axis=1, tiled=True),
            jnp.int32(0),
        )
        energy_rows.append(energy_now)
    stacked = jnp.stack(energy_rows)
    stacked = stacked / (V * OG * V)
    pair_energy = lax.psum(stacked, "virt")
    return (pair_energy, total_grad.reshape(groups_rows, slab_width, naux_width))


CORES = 2


def split_hi_lo(values):
    high = values.astype(jnp.bfloat16)
    low = (values - high.astype(jnp.float32)).astype(jnp.bfloat16)
    return high, low


def pair_kernel(half, energies_ref, own_ref, near_ref, far_ref, left_ref, right_ref, *rest):
    carried_ref = rest[0] if len(rest) == 8 else None
    grad_ref, energy_ref, own_wide, mate_wide, mate_tall, amp_wide, total = rest[-7:]
    row, step = pl.program_id(0), pl.program_id(1)
    steps = pl.num_programs(1)
    virt_width, naux_width = total.shape
    depth = naux_width

    def hold_mate(mate):
        high, low = split_hi_lo(mate)
        mate_wide[step, :, :depth] = high
        mate_wide[step, :, depth : 2 * depth] = high
        mate_wide[step, :, 2 * depth :] = low
        mate_tall[step, :virt_width] = high
        mate_tall[step, virt_width : 2 * virt_width] = high
        mate_tall[step, 2 * virt_width :] = low

    @pl.when((row == 0) & (step < half))
    def _():
        hold_mate(near_ref[0])

    @pl.when((row == 0) & (step >= half))
    def _():
        hold_mate(far_ref[0])

    @pl.when(step == 0)
    def _():
        high, low = split_hi_lo(own_ref[0])
        own_wide[:, :depth] = high
        own_wide[:, depth : 2 * depth] = low
        own_wide[:, 2 * depth :] = high
        if carried_ref is None:
            total[...] = jnp.zeros_like(total)
        else:
            total[...] = carried_ref[0]

    coulomb = lax.dot_general(
        own_wide[...],
        mate_wide[step],
        (((1,), (1,)), ((), ())),
        preferred_element_type=jnp.float32,
    )
    own_energy = energies_ref[0, row]
    mate_energy = energies_ref[1, step]
    denominator = left_ref[...] + right_ref[...] - own_energy - mate_energy
    amplitude = (coulomb.T - 2.0 * coulomb) / denominator
    energy_ref[0, 0] = (amplitude * coulomb).reshape(virt_width // 8, 8, virt_width).sum(0)
    high, low = split_hi_lo(amplitude)
    amp_wide[:, :virt_width] = high
    amp_wide[:, virt_width : 2 * virt_width] = low
    amp_wide[:, 2 * virt_width :] = high
    total[...] += jnp.dot(amp_wide[...], mate_tall[step], preferred_element_type=jnp.float32)

    @pl.when(step == steps - 1)
    def _():
        grad_ref[0] = total[...]


def pair_rows(own, first, rows, near, far, own_energy, mate_energy, virt_energy, carried):
    _, virt_width, naux_width = own.shape
    half = near.shape[0]
    steps = 2 * half
    width = max(rows, steps)
    energies = jnp.stack(
        [
            jnp.pad(own_energy[first : first + rows], (0, width - rows)),
            jnp.pad(mate_energy, (0, width - steps)),
        ]
    )
    block = (1, virt_width, naux_width)

    def near_map(i, s, e):
        return jnp.where(i == 0, jnp.minimum(s, half - 1), half - 1), 0, 0

    def far_map(i, s, e):
        return jnp.where(i == 0, jnp.maximum(s - half, 0), half - 1), 0, 0

    def own_map(i, s, e):
        return first + i, 0, 0

    in_specs = [
        pl.BlockSpec(block, own_map),
        pl.BlockSpec(block, near_map),
        pl.BlockSpec(block, far_map),
        pl.BlockSpec((virt_width, 1), lambda i, s, e: (0, 0)),
        pl.BlockSpec((1, virt_width), lambda i, s, e: (0, 0)),
    ]
    operands = [own, near, far, virt_energy[:, None], virt_energy[None, :]]
    if carried is not None:
        in_specs.append(pl.BlockSpec(block, own_map))
        operands.append(carried)
    flops = 2 * 2 * 3 * rows * steps * virt_width * virt_width * naux_width
    grad, energy = pl.pallas_call(
        functools.partial(pair_kernel, half),
        grid_spec=pltpu.PrefetchScalarGridSpec(
            num_scalar_prefetch=1,
            grid=(rows, steps),
            in_specs=in_specs,
            out_specs=[
                pl.BlockSpec(block, lambda i, s, e: (i, 0, 0)),
                pl.BlockSpec((1, 1, 8, virt_width), lambda i, s, e: (i, s, 0, 0)),
            ],
            scratch_shapes=[
                pltpu.VMEM((virt_width, 3 * naux_width), jnp.bfloat16),
                pltpu.VMEM((steps, virt_width, 3 * naux_width), jnp.bfloat16),
                pltpu.VMEM((steps, 3 * virt_width, naux_width), jnp.bfloat16),
                pltpu.VMEM((virt_width, 3 * virt_width), jnp.bfloat16),
                pltpu.VMEM((virt_width, naux_width), jnp.float32),
            ],
        ),
        out_shape=[
            jax.ShapeDtypeStruct((rows, virt_width, naux_width), jnp.float32),
            jax.ShapeDtypeStruct((rows, steps, 8, virt_width), jnp.float32),
        ],
        cost_estimate=pl.CostEstimate(flops=flops, bytes_accessed=2**24, transcendentals=0),
        name="pair_rows",
    )(energies, *operands)
    return grad, energy.sum((1, 2, 3))


def exchange_pieces(pieces, group_index, group_count):
    arrived = lax.dynamic_update_index_in_dim(
        jnp.zeros_like(pieces), lax.dynamic_index_in_dim(pieces, group_index, 0), group_index, 0
    )
    for shift in range(1, group_count):
        sent = lax.dynamic_index_in_dim(pieces, lax.rem(group_index + shift, group_count), 0)
        got = lax.ppermute(
            sent, "occ", [(s, (s + shift) % group_count) for s in range(group_count)]
        )
        source = lax.rem(group_index + group_count - shift, group_count)
        arrived = lax.dynamic_update_index_in_dim(arrived, got, source, 0)
    return arrived


def per_device(factors, occ_energy, virt_energy, pairing):
    group_index = lax.axis_index("occ")
    column_index = lax.axis_index("virt")
    group_count = lax.axis_size("occ")
    virt_count = lax.axis_size("virt")
    groups_rows, virt_width, naux_width = factors.shape
    if groups_rows % virt_count or virt_count % CORES or pairing.shape[0] != 2:
        return per_device_slabs(factors, occ_energy, virt_energy, pairing)
    span = virt_count // CORES
    place, core = column_index // CORES, column_index % CORES
    half = groups_rows // virt_count
    own_count = groups_rows // CORES
    slab = virt_width // virt_count
    twin = [(v, v ^ 1) for v in range(virt_count)]

    share = lax.dynamic_slice_in_dim(factors, column_index * half, half, 0)
    own = lax.dynamic_slice_in_dim(factors, core * own_count, own_count, 0)
    pieces = share.reshape(group_count, half * virt_width // group_count, naux_width)
    mixed = lax.all_to_all(pieces, "occ", split_axis=0, concat_axis=0, tiled=True)
    shape = (half, virt_width, naux_width)
    first = jnp.take(mixed, pairing[0], axis=0)
    near_0 = lax.all_to_all(first, "occ", split_axis=0, concat_axis=0, tiled=True).reshape(shape)
    far_0 = lax.ppermute(near_0, "virt", twin)
    mixed_late, _ = lax.optimization_barrier((mixed, near_0))
    second = jnp.take(mixed_late, pairing[1], axis=0)
    near_1 = exchange_pieces(second, group_index, group_count).reshape(shape)
    far_1 = lax.ppermute(near_1, "virt", twin)

    grouped = occ_energy.reshape(group_count, groups_rows)
    own_energy = lax.dynamic_slice_in_dim(grouped[group_index], core * own_count, own_count, 0)

    def energy_of_mates(round_index):
        mate = grouped[pairing[round_index, group_index]]
        near_part = lax.dynamic_slice_in_dim(mate, column_index * half, half, 0)
        far_part = lax.dynamic_slice_in_dim(
            mate, (place * CORES + 1 - core) * half, half, 0
        )
        return jnp.concatenate([near_part, far_part])

    mates_0 = energy_of_mates(0)
    carried, energy_0 = pair_rows(
        own, 0, own_count, near_0, far_0, own_energy, mates_0, virt_energy, None
    )
    mates_1 = energy_of_mates(1)
    sizes = [own_count - own_count // 2] + [1] * (own_count // 2)
    start, energy_1, mine, theirs = 0, [], [], []
    for rows in sizes:
        grad, energy = pair_rows(
            own, start, rows, near_1, far_1, own_energy, mates_1, virt_energy, carried
        )
        start += rows
        energy_1.append(energy)
        parts = grad.reshape(rows, span, CORES * slab, naux_width)
        kept = lax.dynamic_index_in_dim(parts, place, 1, keepdims=False)
        for shift in range(1, span):
            sent = lax.dynamic_index_in_dim(parts, lax.rem(place + shift, span), 1, keepdims=False)
            kept = kept + lax.ppermute(
                sent,
                "virt",
                [(v, (v + shift * CORES) % virt_count) for v in range(virt_count)],
            )
        mine.append(lax.dynamic_slice_in_dim(kept, core * slab, slab, 1))
        theirs.append(
            lax.ppermute(
                lax.dynamic_slice_in_dim(kept, (1 - core) * slab, slab, 1), "virt", twin
            )
        )
    mine, theirs = jnp.concatenate(mine), jnp.concatenate(theirs)
    gradient = jnp.where(
        core == 0, jnp.concatenate([mine, theirs]), jnp.concatenate([theirs, mine])
    )
    energies = jnp.stack([energy_0, jnp.concatenate(energy_1)])
    energies = energies / (virt_width * groups_rows * virt_width)
    placed = lax.dynamic_update_slice_in_dim(
        jnp.zeros((2, groups_rows), jnp.float32), energies, core * own_count, 1
    )
    return lax.psum(placed, "virt"), gradient


def solution(mesh):
    placed = (P("occ", None, None), P(), P(), P())

    return jax.shard_map(
        per_device,
        mesh=mesh,
        in_specs=placed,
        out_specs=(P(None, "occ"), P("occ", "virt", None)),
        check_vma=False,
    )
```

```python
import functools

import jax
import jax.numpy as jnp
from jax import lax
from jax.experimental import pallas as pl
from jax.experimental.pallas import tpu as pltpu
from jax.sharding import PartitionSpec as P

OG = 8
V = 512
ROUNDS = 2


def block_amplitude(
    own_rows, mate_rows, own_piece, fragment, own_energy, mate_energy, energy_left, energy_right
):
    highest = lax.Precision.HIGHEST
    groups_rows, slab_width, naux_width = own_rows.shape
    frag_width = fragment.shape[1]
    contract = (((1,), (1,)), ((), ()))
    coulomb = lax.dot_general(
        own_rows.reshape(groups_rows * slab_width, naux_width),
        fragment.reshape(groups_rows * frag_width, naux_width),
        contract,
        precision=highest,
        preferred_element_type=jnp.float32,
    )
    coulomb = coulomb.reshape(groups_rows, slab_width, groups_rows, frag_width)
    swapped = lax.dot_general(
        own_piece.reshape(groups_rows * frag_width, naux_width),
        mate_rows.reshape(groups_rows * slab_width, naux_width),
        contract,
        precision=highest,
        preferred_element_type=jnp.float32,
    )
    swapped = swapped.reshape(groups_rows, frag_width, groups_rows, slab_width).transpose(
        0, 3, 2, 1
    )
    denominator = (
        energy_left[None, :, None, None]
        + energy_right[None, None, None, :]
        - own_energy[:, None, None, None]
        - mate_energy[None, None, :, None]
    )
    amplitude = -(2.0 * coulomb - swapped) / denominator
    return (amplitude, coulomb)


def block_terms(
    own_rows, mate_rows, own_piece, fragment, own_energy, mate_energy, energy_left, energy_right
):
    highest = lax.Precision.HIGHEST
    groups_rows, slab_width, naux_width = own_rows.shape
    frag_width = fragment.shape[1]
    amplitude, coulomb = block_amplitude(
        own_rows, mate_rows, own_piece, fragment, own_energy, mate_energy, energy_left, energy_right
    )
    energy = jnp.sum(amplitude * coulomb, axis=(1, 2, 3))
    grad_part = jnp.dot(
        amplitude.reshape(groups_rows * slab_width, groups_rows * frag_width),
        fragment.reshape(groups_rows * frag_width, naux_width),
        precision=highest,
        preferred_element_type=jnp.float32,
    )
    return (energy, grad_part)


def route_slab(own_rows, partner_row, group_count):
    groups_rows, slab_width, naux_width = own_rows.shape
    split_rows = own_rows.reshape(group_count, groups_rows * slab_width // group_count, naux_width)
    mixed = lax.all_to_all(split_rows, "occ", split_axis=0, concat_axis=0, tiled=True)
    ordered = jnp.take(mixed, partner_row, axis=0)
    arrived = lax.all_to_all(ordered, "occ", split_axis=0, concat_axis=0, tiled=True)
    return arrived.reshape(groups_rows, slab_width, naux_width)


def per_device_slabs(factors, occ_energy, virt_energy, pairing):
    group_index = lax.axis_index("occ")
    column_index = lax.axis_index("virt")
    group_count = lax.axis_size("occ")
    virt_count = lax.axis_size("virt")
    groups_rows, virt_width, naux_width = factors.shape
    slab_width = virt_width // virt_count
    own_rows = lax.dynamic_slice_in_dim(factors, column_index * slab_width, slab_width, 1)
    own_energy = lax.dynamic_slice_in_dim(occ_energy, group_index * groups_rows, groups_rows, 0)
    energy_left = lax.dynamic_slice_in_dim(virt_energy, column_index * slab_width, slab_width, 0)
    total_grad = jnp.zeros((groups_rows * slab_width, naux_width), jnp.float32)
    energy_rows = []
    for round_index in range(ROUNDS):
        partner_row = pairing[round_index]
        mate_index = partner_row[group_index]
        mate_energy = lax.dynamic_slice_in_dim(occ_energy, mate_index * groups_rows, groups_rows, 0)
        partner_row, mate_energy = (partner_row, mate_energy)
        mate_rows = route_slab(own_rows, partner_row, group_count)

        def fold_step(carry, fragment, offset, mate_rows=mate_rows, mate_energy=mate_energy):
            own_piece, energy_right = (factors, virt_energy)
            energy, grad_part = block_terms(
                own_rows,
                mate_rows,
                own_piece,
                fragment,
                own_energy,
                mate_energy,
                energy_left,
                energy_right,
            )
            return (carry[0] + grad_part, energy)

        total_grad, energy_now = fold_step(
            (total_grad, jnp.zeros((groups_rows,), jnp.float32)),
            lax.all_gather(mate_rows, "virt", axis=1, tiled=True),
            jnp.int32(0),
        )
        energy_rows.append(energy_now)
    stacked = jnp.stack(energy_rows)
    stacked = stacked / (V * OG * V)
    pair_energy = lax.psum(stacked, "virt")
    return (pair_energy, total_grad.reshape(groups_rows, slab_width, naux_width))


CORES = 2


def split_hi_lo(values):
    high = values.astype(jnp.bfloat16)
    low = (values - high.astype(jnp.float32)).astype(jnp.bfloat16)
    return high, low


def pair_kernel(half, energies_ref, base_ref, own_ref, near_ref, far_ref, left_ref, right_ref, *rest):
    carried_ref = rest[0] if len(rest) == 8 else None
    grad_ref, energy_ref, own_wide, mate_wide, mate_tall, amp_wide, total = rest[-7:]
    row, step = pl.program_id(0), pl.program_id(1)
    steps = pl.num_programs(1)
    virt_width, naux_width = total.shape
    depth = naux_width

    def hold_mate(mate):
        high, low = split_hi_lo(mate)
        mate_wide[step, :, :depth] = high
        mate_wide[step, :, depth : 2 * depth] = high
        mate_wide[step, :, 2 * depth :] = low
        mate_tall[step, :virt_width] = high
        mate_tall[step, virt_width : 2 * virt_width] = high
        mate_tall[step, 2 * virt_width :] = low

    @pl.when((row == 0) & (step < half))
    def _():
        hold_mate(near_ref[0])

    @pl.when((row == 0) & (step >= half))
    def _():
        hold_mate(far_ref[0])

    @pl.when(step == 0)
    def _():
        high, low = split_hi_lo(own_ref[0])
        own_wide[:, :depth] = high
        own_wide[:, depth : 2 * depth] = low
        own_wide[:, 2 * depth :] = high
        if carried_ref is None:
            total[...] = jnp.zeros_like(total)
        else:
            total[...] = carried_ref[0]

    coulomb = lax.dot_general(
        own_wide[...],
        mate_wide[step],
        (((1,), (1,)), ((), ())),
        preferred_element_type=jnp.float32,
    )
    own_energy = energies_ref[0, row]
    mate_energy = energies_ref[1, step]
    denominator = left_ref[...] + right_ref[...] - own_energy - mate_energy
    amplitude = (coulomb.T - 2.0 * coulomb) / denominator
    energy_ref[0, 0] = (amplitude * coulomb).reshape(virt_width // 8, 8, virt_width).sum(0)
    high, low = split_hi_lo(amplitude)
    amp_wide[:, :virt_width] = high
    amp_wide[:, virt_width : 2 * virt_width] = low
    amp_wide[:, 2 * virt_width :] = high
    total[...] += jnp.dot(amp_wide[...], mate_tall[step], preferred_element_type=jnp.float32)

    @pl.when(step == steps - 1)
    def _():
        grad_ref[0] = total[...]


def pair_rows(own, base, first, rows, near, far, own_energy, mate_energy, virt_energy, carried):
    _, virt_width, naux_width = own.shape
    half = near.shape[0]
    steps = 2 * half
    width = max(rows, steps)
    energies = jnp.stack(
        [
            jnp.pad(own_energy[first : first + rows], (0, width - rows)),
            jnp.pad(mate_energy, (0, width - steps)),
        ]
    )
    block = (1, virt_width, naux_width)

    def near_map(i, s, e, b):
        return jnp.where(i == 0, jnp.minimum(s, half - 1), half - 1), 0, 0

    def far_map(i, s, e, b):
        return jnp.where(i == 0, jnp.maximum(s - half, 0), half - 1), 0, 0

    def own_map(i, s, e, b):
        return b[0] + first + i, 0, 0

    def carried_map(i, s, e, b):
        return first + i, 0, 0

    in_specs = [
        pl.BlockSpec(block, own_map),
        pl.BlockSpec(block, near_map),
        pl.BlockSpec(block, far_map),
        pl.BlockSpec((virt_width, 1), lambda i, s, e, b: (0, 0)),
        pl.BlockSpec((1, virt_width), lambda i, s, e, b: (0, 0)),
    ]
    operands = [own, near, far, virt_energy[:, None], virt_energy[None, :]]
    if carried is not None:
        in_specs.append(pl.BlockSpec(block, carried_map))
        operands.append(carried)
    flops = 2 * 2 * 3 * rows * steps * virt_width * virt_width * naux_width
    grad, energy = pl.pallas_call(
        functools.partial(pair_kernel, half),
        grid_spec=pltpu.PrefetchScalarGridSpec(
            num_scalar_prefetch=2,
            grid=(rows, steps),
            in_specs=in_specs,
            out_specs=[
                pl.BlockSpec(block, lambda i, s, e, b: (i, 0, 0)),
                pl.BlockSpec((1, 1, 8, virt_width), lambda i, s, e, b: (i, s, 0, 0)),
            ],
            scratch_shapes=[
                pltpu.VMEM((virt_width, 3 * naux_width), jnp.bfloat16),
                pltpu.VMEM((steps, virt_width, 3 * naux_width), jnp.bfloat16),
                pltpu.VMEM((steps, 3 * virt_width, naux_width), jnp.bfloat16),
                pltpu.VMEM((virt_width, 3 * virt_width), jnp.bfloat16),
                pltpu.VMEM((virt_width, naux_width), jnp.float32),
            ],
        ),
        out_shape=[
            jax.ShapeDtypeStruct((rows, virt_width, naux_width), jnp.float32),
            jax.ShapeDtypeStruct((rows, steps, 8, virt_width), jnp.float32),
        ],
        cost_estimate=pl.CostEstimate(flops=flops, bytes_accessed=2**24, transcendentals=0),
        name="pair_rows",
    )(energies, base, *operands)
    return grad, energy.sum((1, 2, 3))


def exchange_pieces(pieces, group_index, group_count):
    arrived = lax.dynamic_update_index_in_dim(
        jnp.zeros_like(pieces), lax.dynamic_index_in_dim(pieces, group_index, 0), group_index, 0
    )
    for shift in range(1, group_count):
        sent = lax.dynamic_index_in_dim(pieces, lax.rem(group_index + shift, group_count), 0)
        got = lax.ppermute(
            sent, "occ", [(s, (s + shift) % group_count) for s in range(group_count)]
        )
        source = lax.rem(group_index + group_count - shift, group_count)
        arrived = lax.dynamic_update_index_in_dim(arrived, got, source, 0)
    return arrived


def per_device(factors, occ_energy, virt_energy, pairing):
    group_index = lax.axis_index("occ")
    column_index = lax.axis_index("virt")
    group_count = lax.axis_size("occ")
    virt_count = lax.axis_size("virt")
    groups_rows, virt_width, naux_width = factors.shape
    if groups_rows % virt_count or virt_count != 2 * CORES or pairing.shape[0] != 2:
        return per_device_slabs(factors, occ_energy, virt_energy, pairing)
    span = virt_count // CORES
    place, core = column_index // CORES, column_index % CORES
    half = groups_rows // virt_count
    own_count = groups_rows // CORES
    slab = virt_width // virt_count
    twin = [(v, v ^ 1) for v in range(virt_count)]

    share = lax.dynamic_slice_in_dim(factors, column_index * half, half, 0)
    base = (core * own_count).astype(jnp.int32)[None]
    pieces = share.reshape(group_count, half * virt_width // group_count, naux_width)
    mixed = lax.all_to_all(pieces, "occ", split_axis=0, concat_axis=0, tiled=True)
    shape = (half, virt_width, naux_width)
    first = mixed.at[pairing[0]].get(mode="promise_in_bounds")
    near_0 = exchange_pieces(first, group_index, group_count).reshape(shape)
    far_0 = lax.ppermute(near_0, "virt", twin)
    mixed_late, _ = lax.optimization_barrier((mixed, near_0))
    second = mixed_late.at[pairing[1]].get(mode="promise_in_bounds")
    near_1 = exchange_pieces(second, group_index, group_count).reshape(shape)
    far_1 = lax.ppermute(near_1, "virt", twin)

    grouped = occ_energy.reshape(group_count, groups_rows)
    own_energy = lax.dynamic_slice_in_dim(grouped[group_index], core * own_count, own_count, 0)

    def energy_of_mates(round_index):
        mate = grouped[pairing[round_index, group_index]]
        near_part = lax.dynamic_slice_in_dim(mate, column_index * half, half, 0)
        far_part = lax.dynamic_slice_in_dim(
            mate, (place * CORES + 1 - core) * half, half, 0
        )
        return jnp.concatenate([near_part, far_part])

    mates_0 = energy_of_mates(0)
    carried, energy_0 = pair_rows(
        factors, base, 0, own_count, near_0, far_0, own_energy, mates_0, virt_energy, None
    )
    mates_1 = energy_of_mates(1)
    sizes = [own_count - own_count // 2] + [1] * (own_count // 2)
    start, energy_1, mine, theirs = 0, [], [], []
    for rows in sizes:
        grad, energy = pair_rows(
            factors, base, start, rows, near_1, far_1, own_energy, mates_1, virt_energy, carried
        )
        start += rows
        near_1, far_1, grad = lax.optimization_barrier((near_1, far_1, grad))
        energy_1.append(energy)
        parts = grad.reshape(rows, span, CORES * slab, naux_width)
        kept = lax.dynamic_index_in_dim(parts, place, 1, keepdims=False)
        for shift in range(1, span):
            sent = lax.dynamic_index_in_dim(parts, lax.rem(place + shift, span), 1, keepdims=False)
            got = lax.ppermute(
                sent,
                "virt",
                [(v, (v + shift * CORES) % virt_count) for v in range(virt_count)],
            )
            kept = kept + got
        mine.append(lax.dynamic_slice_in_dim(kept, core * slab, slab, 1))
        theirs.append(
            lax.ppermute(
                lax.dynamic_slice_in_dim(kept, (1 - core) * slab, slab, 1), "virt", twin
            )
        )
    gradient = jnp.zeros((groups_rows, slab, naux_width), jnp.float32)
    start = 0
    for mine_part, their_part in zip(mine, theirs):
        gradient = lax.dynamic_update_slice_in_dim(
            gradient, mine_part, core * own_count + start, 0
        )
        gradient = lax.dynamic_update_slice_in_dim(
            gradient, their_part, (1 - core) * own_count + start, 0
        )
        start += mine_part.shape[0]
    energies = jnp.stack([energy_0, jnp.concatenate(energy_1)])
    energies = energies / (virt_width * groups_rows * virt_width)
    summed = energies
    for shift in range(1, span):
        summed = summed + lax.ppermute(
            energies, "virt", [(v, (v + shift * CORES) % virt_count) for v in range(virt_count)]
        )
    other = lax.ppermute(summed, "virt", twin)
    pair_energy = jnp.where(
        core == 0,
        jnp.concatenate([summed, other], axis=1),
        jnp.concatenate([other, summed], axis=1),
    )
    return pair_energy, gradient


def solution(mesh):
    placed = (P("occ", None, None), P(), P(), P())

    return jax.shard_map(
        per_device,
        mesh=mesh,
        in_specs=placed,
        out_specs=(P(None, "occ"), P("occ", "virt", None)),
        check_vma=False,
    )
```
